256 devices in a mesh: dp: 32 (over x, z), mp: 8 (over y, core).
Axes of the slice: x: 4, y: 4, z: 8, core: 2. Of those that a mesh axis runs over, the one named last changes fastest.
Arguments:
- grads: bfloat16 [32768, 16384], P('dp', 'mp'), may hold values from -6 to 6
- scales: float32 [128, 32768], P('mp', 'dp'), may hold values from 0.25 to 4
- example_group: int32 [32, 1024], P('dp'), may hold values from 0 to 127, never falling along the last dimension, each value on 1 to 32 neighbouring positions
- group_slot: int32 [4096], P('dp'), may hold values from 0 to 4095, as said below
- inv_hess: bfloat16 [16384, 16384], P('mp', 'dp'), may hold values from -0.046875 to 0.046875
- queries: bfloat16 [1024, 16384], P(None, 'mp'), may hold values from -0.029907227 to 0.029907227
Outputs:
- scores: float32 [4096, 1024], P('dp', 'mp')
The draws below stay inside these ranges and needn't reach their ends.
Inputs may be any that keep to these rules, and one draw needn't show every extreme that they name: `group_slot`: A permutation of the 4096 rows. The groups of one block of 128 (one index of dp) put at most 8 groups into the rows of any one owner block of 128 output rows, and exactly 8 into some owner block.
All inputs are finite; a program needn't handle non-finite values.
Results may differ from the reference program's by a relative error of at most 0.0049.
Values may be sent and summed in bfloat16 or wider, within the bound.
A program may use at most 64 MiB of HBM per device.

```python
import math
import jax
import jax.numpy as jnp
import numpy as np
from jax import lax

P_SIZE = 16384
QBLOCK = 128
GRP_DEV = 128
EX_DEV = 1024
GROUPS = 4096
EXAMPLES = 32768
NQ = 1024
N_DP = 32


def draw_group_slot(key, part):
    per_owner = GRP_DEV // N_DP
    first, second = jax.random.split(jax.random.fold_in(key, 11))
    leading = jax.random.permutation(first, N_DP)
    trailing = jnp.roll(leading, -1)
    owners = jnp.arange(N_DP, dtype=jnp.int32)
    counts = per_owner + per_owner * (owners[None, :] == leading[:, None]).astype(jnp.int32) - per_owner * (owners[None, :] == trailing[:, None]).astype(jnp.int32)
    ends = jnp.cumsum(counts, axis=1)
    starts = ends - counts
    offsets = jnp.cumsum(counts, axis=0) - counts
    row_keys = jax.random.split(second, N_DP)
    shuffles = jax.vmap(lambda one_key: jax.random.permutation(one_key, GRP_DEV))(row_keys)
    position = jnp.arange(GRP_DEV, dtype=jnp.int32)
    target = jnp.sum((position[None, :, None] >= ends[:, None, :]).astype(jnp.int32), axis=2)
    within = position[None, :] - jnp.take_along_axis(starts, target, axis=1)
    slot_at = target * GRP_DEV + jnp.take_along_axis(offsets, target, axis=1) + within
    placing = jnp.argsort(shuffles, axis=1)
    by_group = jnp.take_along_axis(slot_at, placing, axis=1)
    return by_group.reshape(-1).astype(jnp.int32)


def block_scale(own_key, dims, shards, low, high):
    def one(dim, blocks):
        steps = jax.random.uniform(jax.random.fold_in(jax.random.fold_in(own_key, 6), dim), (blocks,), jnp.float32, low / len(shards), high / len(shards))
        return jnp.repeat(jnp.exp(steps), dims[dim] // blocks).reshape((-1,) + (1,) * (len(dims) - dim - 1))

    factor_of = one(*shards[0])
    for cut in shards[1:]:
        factor_of = factor_of * one(*cut)
    return factor_of


def split_up(amount, total, most, lean):
    weights = [(1 << 20) // math.isqrt(standing ** lean) + 1 for standing in range(2, amount + 1)]
    spare, given = total - most - (amount - 1), [1] * (amount - 1)
    while spare > 0:
        candidates = [i for i in range(amount - 1) if given[i] < most]
        pool, remaining = sum([weights[i] for i in candidates]), spare
        for i in candidates:
            addition = min(most - given[i], max(1, remaining * weights[i] // pool), spare)
            given[i] = given[i] + addition
            spare = spare - addition
    return np.array([most] + given)


def uneven_parts(key, amount, total, reach, skew):
    if amount == 2:
        one = jax.random.randint(key, (), max(1, total - reach), min(reach, total - 1) + 1)
        return jnp.stack([one, total - one])
    lengths = jnp.asarray(split_up(amount, total, reach, skew), jnp.int32)
    couples = (amount - 1) // 2
    source_of, sink = lengths[1:1 + 2 * couples:2], lengths[2:2 + 2 * couples:2]
    margin = jnp.minimum(source_of - 1, reach - sink)
    passed = jax.random.randint(jax.random.fold_in(key, 1), (couples,), 0, 1 << 20) % (margin + 1)
    lengths = lengths.at[1:1 + 2 * couples:2].set(source_of - passed).at[2:2 + 2 * couples:2].set(sink + passed)
    return lengths[jax.random.permutation(jax.random.fold_in(key, 2), amount)]


def centred(rng, dims, spread, reach, cuts=(), held_as=jnp.bfloat16):
    array = spread * jax.random.normal(rng, dims, jnp.float32)
    if cuts:
        array = array * block_scale(rng, dims, cuts, -0.22, 0.18)
    return jnp.clip(array, -reach, reach).astype(held_as)


def setup_inputs(seed: int = 0) -> dict:
    seeds = jax.random.split(jax.random.key(seed), 7)
    grads = centred(seeds[0], (EXAMPLES, P_SIZE), 1.0, 6.0, ((0, 32), (1, 8)))
    scales = jnp.clip(jnp.exp(math.log(4.0) - 2.7725887 * jax.random.uniform(seeds[1], (P_SIZE // QBLOCK, EXAMPLES), jnp.float32) ** block_scale(seeds[1], (P_SIZE // QBLOCK, EXAMPLES), ((0, 8), (1, 32)), -0.2, 0.2)), 0.25, 4.0)
    example_group = jax.vmap(lambda own: jnp.searchsorted(jnp.cumsum(uneven_parts(own, GRP_DEV, EX_DEV, 4 * EX_DEV // GRP_DEV, 2)), jnp.arange(EX_DEV), side="right"))(jax.random.split(seeds[2], N_DP)).reshape((N_DP, EX_DEV)).astype(jnp.int32)
    group_slot = draw_group_slot(jax.random.fold_in(seeds[6], 71), 0)
    inv_hess = centred(seeds[4], (P_SIZE, P_SIZE), P_SIZE ** -0.5, 0.046875, ((0, 8), (1, 32)))
    queries = centred(seeds[5], (NQ, P_SIZE), 0.005, 0.029907227, ((1, 8),))
    return {"grads": grads, "scales": scales, "example_group": example_group, "group_slot": group_slot, "inv_hess": inv_hess, "queries": queries}


def block_sums(pieces):
    rows, block_scales, members = pieces
    dequant = (rows.reshape(EX_DEV, P_SIZE // QBLOCK, QBLOCK) * jnp.transpose(block_scales)[:, :, None]).astype(jnp.bfloat16).reshape(EX_DEV, P_SIZE)
    onehot = (jnp.arange(GRP_DEV, dtype=jnp.int32)[:, None] == members[None, :]).astype(jnp.bfloat16)
    return jnp.dot(onehot, dequant, preferred_element_type=jnp.float32).astype(jnp.bfloat16)


def reference(grads, scales, example_group, group_slot, inv_hess, queries):
    grad_blocks = grads.reshape(N_DP, EX_DEV, P_SIZE)
    scale_blocks = jnp.transpose(scales.reshape(P_SIZE // QBLOCK, N_DP, EX_DEV), (1, 0, 2))
    group_grad = lax.map(block_sums, (grad_blocks, scale_blocks, example_group)).reshape(GROUPS, P_SIZE)
    precond = jnp.dot(queries, inv_hess, preferred_element_type=jnp.float32).astype(jnp.bfloat16)
    raw = lax.dot_general(group_grad, precond, (((1,), (1,)), ((), ())), preferred_element_type=jnp.float32)
    scores = jnp.zeros((GROUPS, NQ), jnp.float32).at[group_slot.astype(jnp.int32)].set(raw)
    return scores
```

```python
import functools

import jax
import jax.numpy as jnp
from jax import lax
from jax.experimental import pallas as pl
from jax.experimental.pallas import tpu as pltpu
from jax.sharding import PartitionSpec as P

MESH = pl.DeviceIdType.MESH
BF16, F32, I32 = jnp.bfloat16, jnp.float32, jnp.int32
NX, NY, NZ = 4, 4, 8
KCH = 2
CW = 256


def dev(x, y, z, c):
    return (lax.rem(x, NX) * NZ + lax.rem(z, NZ), lax.rem(y, NY) * 2 + c)


def kernel(
    grads_ref, sct_ref, member_ref, slot_ref, hess_ref, query_ref, out_ref,
    q_v, h_v, g_v, ex_s, ex_r, own, rs_s, rs_r, tr_s, pre, gall, acc, slots, slot_rep, pack, place, a2a_s, a2a_r,
    in_sem, ex_sem, rs_sem, rr_sem, tr_sem, agr_sem, agl_sem, gr_sem, gl_sem, gf_sem, gp_sem, sl_sem, slr_sem, as_sem, ar_sem,
):
    d = lax.axis_index("dp")
    m = lax.axis_index("mp")
    x, z = lax.div(d, NZ), lax.rem(d, NZ)
    y, c = lax.div(m, 2), lax.rem(m, 2)
    oc = 1 - c
    beta = lax.rem(2 * y - x + NX, NX)
    stays = (x == y).astype(I32)

    def q_copy(i, b):
        h = oc if i == 0 else c
        rows = pl.ds(pl.multiple_of(b * 256 + h * 128, 128), 128)
        return pltpu.make_async_copy(query_ref.at[rows], q_v.at[i, b], in_sem.at[i * 4 + b])

    def h_copy(k):
        return pltpu.make_async_copy(hess_ref.at[:, pl.ds(k * CW, CW)], h_v.at[k], in_sem.at[8 + k])

    def g_copy(i):
        return pltpu.make_async_copy(grads_ref.at[:, pl.ds(i * 1024, 1024)], g_v.at[i], in_sem.at[10 + i])

    h_copy(0).start()
    for b in range(4):
        q_copy(0, b).start()
    for b in range(4):
        q_copy(1, b).start()
    h_copy(1).start()
    g_copy(0).start()
    g_copy(1).start()

    barrier = pltpu.get_barrier_semaphore()

    def greet(target):
        pl.semaphore_signal(barrier, inc=1, device_id=target, device_id_type=MESH)

    greet(dev(x, y, z, oc))
    for o in (1, 2, 3):
        greet(dev(x, y + o, z, c))
    greet(dev(x + 1, y, z, c))
    greet(dev(x + 3, y, z, c))
    greet(dev(x, y, z + 1, c))
    greet(dev(x, y, z + 7, c))

    def owner_of(o):
        return dev(lax.div(o, NZ), beta, lax.rem(o, NZ), c)

    def source_of(s):
        ys, zs = lax.div(s, NZ), lax.rem(s, NZ)
        return dev(2 * ys - y + NX, ys, zs, c)

    own_src = y * NZ + z
    me_owner = jnp.where(stays == 1, d, -1)
    me_source = jnp.where(stays == 1, own_src, -1)

    def greet_32(i, carry):
        @pl.when(i != me_owner)
        def _():
            greet(owner_of(i))

        @pl.when(i != me_source)
        def _():
            greet(source_of(i))

        return carry

    lax.fori_loop(0, 32, greet_32, 0)

    def partial(i, k):
        return jnp.dot(q_v[i].reshape(512, 2048), h_v[k], preferred_element_type=F32)

    def ex_copy(k):
        return pltpu.make_async_remote_copy(
            src_ref=ex_s.at[k], dst_ref=ex_r.at[k], send_sem=ex_sem.at[0, k], recv_sem=ex_sem.at[1, k],
            device_id=dev(x, y, z, oc), device_id_type=MESH)

    h_copy(0).wait()
    for b in range(4):
        q_copy(0, b).wait()
    ex_s[0] = partial(0, 0).astype(BF16).reshape(4, 128, CW)
    pl.semaphore_wait(barrier, 72 - 2 * stays)
    ex_copy(0).start()
    for b in range(4):
        q_copy(1, b).wait()
    own[0] = partial(1, 0).reshape(4, 128, CW)
    h_copy(1).wait()
    ex_s[1] = partial(0, 1).astype(BF16).reshape(4, 128, CW)
    ex_copy(1).start()

    def rs_copy(k, o):
        b = lax.rem(y + o, NY)
        return pltpu.make_async_remote_copy(
            src_ref=rs_s.at[k, b], dst_ref=rs_r.at[k, y], send_sem=rs_sem.at[k, o], recv_sem=rr_sem.at[k, y],
            device_id=dev(x, y + o, z, c), device_id_type=MESH)

    def rs_wait_recv(k, o):
        s = lax.rem(y + o, NY)
        pltpu.make_async_remote_copy(
            src_ref=rs_s.at[k, s], dst_ref=rs_r.at[k, s], send_sem=rs_sem.at[k, o], recv_sem=rr_sem.at[k, s],
            device_id=dev(x, y + o, z, c), device_id_type=MESH).wait_recv()

    def rs_send(k):
        ex_copy(k).wait_recv()
        for o in (2, 1, 3):
            b = lax.rem(y + o, NY)
            rs_s[k, b] = (own[k, b] + ex_r[k, b].astype(F32)).astype(BF16)
            rs_copy(k, o).start()

    rs_send(0)
    own[1] = partial(1, 1).reshape(4, 128, CW)
    rs_send(1)

    def slot_copy(s):
        return pltpu.make_async_remote_copy(
            src_ref=slot_ref, dst_ref=slots.at[d], send_sem=sl_sem.at[s], recv_sem=slr_sem.at[d],
            device_id=source_of(s), device_id_type=MESH)

    def slot_send(s, carry):
        @pl.when(s != me_source)
        def _():
            slot_copy(s).start()

        return carry

    lax.fori_loop(0, 32, slot_send, 0)

    @pl.when(stays == 1)
    def _():
        slots[d] = slot_ref[...]

    onehot = (lax.broadcasted_iota(I32, (128, 1024), 0) == member_ref[...]).astype(F32).astype(BF16)

    def group_half(h):
        g_copy(h).wait()
        for i in range(2):
            for k in range(KCH):
                col = (i * KCH + k) * CW
                parts = []
                for j in range(2):
                    at = col + j * 128
                    blk = (h * 1024 + at) // 128
                    parts.append((g_v[h, :, at : at + 128].astype(F32) * sct_ref[:, blk : blk + 1]).astype(BF16))
                deq = jnp.concatenate(parts, axis=1)
                gall[x, 4 * c + 2 * h + i, k] = jnp.dot(onehot, deq, preferred_element_type=F32).astype(BF16)

    def piece(xx, cc, h):
        return gall.at[lax.rem(xx, NX), pl.ds(4 * cc + 2 * h, 2)]

    def g_right(h):
        return pltpu.make_async_remote_copy(
            src_ref=piece(x, c, h), dst_ref=piece(x, c, h), send_sem=gr_sem.at[0, h], recv_sem=gr_sem.at[1, h],
            device_id=dev(x + 1, y, z, c), device_id_type=MESH)

    def g_left(h):
        return pltpu.make_async_remote_copy(
            src_ref=piece(x, c, h), dst_ref=piece(x, c, h), send_sem=gl_sem.at[0, h], recv_sem=gl_sem.at[1, h],
            device_id=dev(x + 3, y, z, c), device_id_type=MESH)

    def g_forward(h):
        src = piece(x + 3, c, 0) if h == 0 else piece(x + 1, c, 1)
        to = dev(x + 1, y, z, c) if h == 0 else dev(x + 3, y, z, c)
        return pltpu.make_async_remote_copy(
            src_ref=src, dst_ref=src, send_sem=gf_sem.at[0, h], recv_sem=gf_sem.at[1, h], device_id=to, device_id_type=MESH)

    def g_partner(o, h):
        return pltpu.make_async_remote_copy(
            src_ref=piece(x + o, c, h), dst_ref=piece(x + o, c, h), send_sem=gp_sem.at[0, o, h], recv_sem=gp_sem.at[1, o, h],
            device_id=dev(x, y, z, oc), device_id_type=MESH)

    def g_send(h):
        g_right(h).start()
        g_left(h).start()
        g_partner(0, h).start()

    group_half(0)
    g_send(0)

    def tr_copy(k):
        return pltpu.make_async_remote_copy(
            src_ref=tr_s.at[k], dst_ref=pre.at[k, z], send_sem=tr_sem.at[0, k], recv_sem=tr_sem.at[1, k],
            device_id=dev(2 * x - y + NX, x, z, c), device_id_type=MESH)

    def tr_send(k):
        total = own[k, y] + ex_r[k, y].astype(F32)
        for o in (1, 3, 2):
            rs_wait_recv(k, o)
            total += rs_r[k, lax.rem(y + o, NY)].astype(F32)
        tr_s[k] = total.astype(BF16)

        @pl.when(stays == 0)
        def _():
            tr_copy(k).start()

        @pl.when(stays == 1)
        def _():
            pre[k, z] = total.astype(BF16)

    tr_send(0)
    group_half(1)
    tr_send(1)
    g_send(1)

    def ag_copy(k, s, right):
        sems = agr_sem if right else agl_sem
        blk = lax.rem(z - s + NZ, NZ) if right else lax.rem(z + s, NZ)
        return pltpu.make_async_remote_copy(
            src_ref=pre.at[k, blk], dst_ref=pre.at[k, blk], send_sem=sems.at[0, k, s], recv_sem=sems.at[1, k, s],
            device_id=dev(x, y, z + (1 if right else NZ - 1), c), device_id_type=MESH)

    def ag_wait_recv(k, s, right):
        sems = agr_sem if right else agl_sem
        blk = lax.rem(z - s - 1 + NZ, NZ) if right else lax.rem(z + s + 1, NZ)
        pltpu.make_async_remote_copy(
            src_ref=pre.at[k, blk], dst_ref=pre.at[k, blk], send_sem=sems.at[0, k, s], recv_sem=sems.at[1, k, s],
            device_id=dev(x, y, z + (1 if right else NZ - 1), c), device_id_type=MESH).wait_recv()

    def steps(k, right):
        return 4 if (k == 0) == right else 3

    for k in range(KCH):
        @pl.when(stays == 0)
        def _():
            tr_copy(k).wait_recv()

        ag_copy(k, 0, True).start()
        ag_copy(k, 0, False).start()

    upper = (lax.broadcasted_iota(I32, (128, 128), 0) < lax.broadcasted_iota(I32, (128, 128), 1)).astype(F32).astype(BF16)

    def slot_wait(o, carry):
        @pl.when(o != me_owner)
        def _():
            pltpu.make_async_remote_copy(
                src_ref=slot_ref, dst_ref=slots.at[o], send_sem=sl_sem.at[o], recv_sem=slr_sem.at[o],
                device_id=source_of(o), device_id_type=MESH).wait_recv()

        return carry

    lax.fori_loop(0, 32, slot_wait, 0)
    row = lax.broadcasted_iota(I32, (1024, 128), 0)
    for xx in range(NX):
        hit = lax.shift_right_logical(slots[xx * NZ + z], 7) == lax.shift_right_logical(row, 5)
        mine = hit & ((lax.shift_right_logical(row, 3) & 3) == xx)
        rank = jnp.dot(hit.astype(F32).astype(BF16), upper, preferred_element_type=F32)
        pack[:, xx * 128 : (xx + 1) * 128] = jnp.where(
            mine & (rank == (row & 7).astype(F32)), 1.0, 0.0).astype(BF16)
    for j in range(32):
        slot_rep[j * 8 : (j + 1) * 8, :] = jnp.broadcast_to(slots[(j % 4) * NZ + j // 4], (8, 128))
    rep = slot_rep[...]
    row = lax.broadcasted_iota(I32, (256, 128), 0)
    hit = lax.shift_right_logical(rep, 7) == d
    rank = jnp.dot(hit.astype(F32).astype(BF16), upper, preferred_element_type=F32)
    taken = jnp.where(hit & (rank == (row & 7).astype(F32)), (rep & 127).astype(F32) + 1.0, 0.0)
    target = jnp.sum(taken, axis=1, keepdims=True) - 1.0
    place[...] = jnp.where(
        target == lax.broadcasted_iota(I32, (256, 128), 1).astype(F32), 1.0, 0.0).astype(BF16)

    def ag_step(s):
        for k in range(KCH):
            for right in (True, False):
                if s < steps(k, right):
                    ag_wait_recv(k, s, right)
                    if s + 1 < steps(k, right):
                        ag_copy(k, s + 1, right).start()

    def g_wait(kind, h):
        src = {"r": (gr_sem, piece(x + 3, c, h)), "l": (gl_sem, piece(x + 1, c, h)), "f": (gf_sem, piece(x + 2, c, h))}
        sems, ref = src[kind]
        pltpu.make_async_remote_copy(
            src_ref=ref, dst_ref=ref, send_sem=sems.at[0, h], recv_sem=sems.at[1, h],
            device_id=dev(x + 1, y, z, c), device_id_type=MESH).wait_recv()

    def gp_wait(o, h):
        ref = piece(x + o, oc, h)
        pltpu.make_async_remote_copy(
            src_ref=ref, dst_ref=ref, send_sem=gp_sem.at[0, o, h], recv_sem=gp_sem.at[1, o, h],
            device_id=dev(x, y, z, oc), device_id_type=MESH).wait_recv()

    g_wait("r", 0)
    g_forward(0).start()
    g_partner(3, 0).start()
    g_wait("l", 0)
    g_partner(1, 0).start()
    ag_step(0)
    ag_step(1)
    g_wait("l", 1)
    g_forward(1).start()
    g_partner(1, 1).start()
    g_wait("r", 1)
    g_partner(3, 1).start()
    ag_step(2)
    g_wait("f", 0)
    g_partner(2, 0).start()
    ag_step(3)

    def multiply(o):
        xx = lax.rem(x + o, NX)

        def body(zz, total):
            for k in range(KCH):
                total += lax.dot_general(
                    gall[xx, zz, k], pre[k, zz], (((1,), (1,)), ((), ())), preferred_element_type=F32)
            return total

        acc[xx] = lax.fori_loop(0, NZ, body, jnp.zeros((128, 128), F32))

    for o in (0, 1, 3):
        gp_wait(o, 0)
        gp_wait(o, 1)
        multiply(o)
    g_wait("f", 1)
    g_partner(2, 1).start()
    gp_wait(2, 0)
    gp_wait(2, 1)
    multiply(2)

    a2a_s[...] = jnp.dot(
        pack[...], acc[...].reshape(512, 128).astype(BF16), preferred_element_type=F32).astype(BF16).reshape(32, 32, 128)

    def out_copy(o):
        return pltpu.make_async_remote_copy(
            src_ref=a2a_s.at[o], dst_ref=a2a_r.at[own_src], send_sem=as_sem.at[o], recv_sem=ar_sem.at[own_src],
            device_id=owner_of(o), device_id_type=MESH)

    def out_send(i, carry):
        o = lax.rem(d + i, 32)

        @pl.when(o != me_owner)
        def _():
            out_copy(o).start()

        return carry

    lax.fori_loop(0, 32, out_send, 0)

    @pl.when(stays == 1)
    def _():
        a2a_r[own_src] = a2a_s[d]

    def out_wait(s, carry):
        @pl.when(s != me_source)
        def _():
            pltpu.make_async_remote_copy(
                src_ref=a2a_s.at[s], dst_ref=a2a_r.at[s], send_sem=as_sem.at[s], recv_sem=ar_sem.at[s],
                device_id=source_of(s), device_id_type=MESH).wait_recv()

        return carry

    lax.fori_loop(0, 32, out_wait, 0)
    total = jnp.zeros((128, 128), F32)
    for ys in range(NY):
        rows = a2a_r[ys * NZ : (ys + 1) * NZ].reshape(256, 128)
        total += lax.dot_general(place[...], rows, (((0,), (0,)), ((), ())), preferred_element_type=F32)
    out_ref[...] = total

    for k in range(KCH):
        ex_copy(k).wait_send()
        for o in (1, 2, 3):
            rs_copy(k, o).wait_send()

        @pl.when(stays == 0)
        def _():
            tr_copy(k).wait_send()

        for right in (True, False):
            for s in range(steps(k, right)):
                ag_copy(k, s, right).wait_send()
    for h in range(2):
        g_right(h).wait_send()
        g_left(h).wait_send()
        g_forward(h).wait_send()
        for o in range(NX):
            g_partner(o, h).wait_send()

    def drain(i, carry):
        @pl.when(i != me_source)
        def _():
            slot_copy(i).wait_send()

        @pl.when(i != me_owner)
        def _():
            out_copy(i).wait_send()

        return carry

    lax.fori_loop(0, 32, drain, 0)


def local(grads, scales, example_group, group_slot, inv_hess, queries):
    vmem = pl.BlockSpec(memory_space=pltpu.VMEM)
    hbm = pl.BlockSpec(memory_space=pl.ANY)
    dma = pltpu.SemaphoreType.DMA
    return pl.pallas_call(
        kernel,
        out_shape=jax.ShapeDtypeStruct((128, 128), F32),
        in_specs=[hbm, vmem, vmem, vmem, hbm, hbm],
        out_specs=vmem,
        scratch_shapes=[
            pltpu.VMEM((2, 4, 128, 2048), BF16),
            pltpu.VMEM((KCH, 2048, CW), BF16),
            pltpu.VMEM((2, 1024, 1024), BF16),
            pltpu.VMEM((KCH, 4, 128, CW), BF16),
            pltpu.VMEM((KCH, 4, 128, CW), BF16),
            pltpu.VMEM((KCH, 4, 128, CW), F32),
            pltpu.VMEM((KCH, 4, 128, CW), BF16),
            pltpu.VMEM((KCH, 4, 128, CW), BF16),
            pltpu.VMEM((KCH, 128, CW), BF16),
            pltpu.VMEM((KCH, NZ, 128, CW), BF16),
            pltpu.VMEM((NX, NZ, KCH, 128, CW), BF16),
            pltpu.VMEM((NX, 128, 128), F32),
            pltpu.VMEM((32, 1, 128), I32),
            pltpu.VMEM((256, 128), I32),
            pltpu.VMEM((1024, 512), BF16),
            pltpu.VMEM((256, 128), BF16),
            pltpu.VMEM((32, 32, 128), BF16),
            pltpu.VMEM((32, 32, 128), BF16),
            dma((12,)),
            dma((2, KCH)),
            dma((KCH, 4)),
            dma((KCH, 4)),
            dma((2, KCH)),
            dma((2, KCH, 4)),
            dma((2, KCH, 4)),
            dma((2, 2)),
            dma((2, 2)),
            dma((2, 2)),
            dma((2, 4, 2)),
            dma((32,)),
            dma((32,)),
            dma((32,)),
            dma((32,)),
        ],
        compiler_params=pltpu.CompilerParams(collective_id=0, has_side_effects=True, vmem_limit_bytes=48 * 2**20),
        name="scores",
    )(grads, jnp.transpose(scales), example_group, group_slot.reshape(1, 128), inv_hess, queries)


def solution(mesh):
    in_specs = (P("dp", "mp"), P("mp", "dp"), P("dp", None), P("dp"), P("mp", "dp"), P(None, "mp"))
    out_specs = P("dp", "mp")
    return jax.shard_map(local, mesh=mesh, in_specs=in_specs, out_specs=out_specs, check_vma=False)
```

```python
import functools

import jax
import jax.numpy as jnp
from jax import lax
from jax.experimental import pallas as pl
from jax.experimental.pallas import tpu as pltpu
from jax.sharding import PartitionSpec as P

MESH = pl.DeviceIdType.MESH
BF16, F32, I32 = jnp.bfloat16, jnp.float32, jnp.int32
NX, NY, NZ = 4, 4, 8
KCH = 2
CW = 256


def dev(x, y, z, c):
    return (lax.rem(x, NX) * NZ + lax.rem(z, NZ), lax.rem(y, NY) * 2 + c)


def kernel(
    grads_ref, scale_ref, member_hbm, slot_hbm, hess_ref, query_ref, out_ref,
    scale_v, sct_ref, member_ref, slot_ref, q_v, h_v, g_v, ex_s, ex_r, own, rs_s, rs_r, tr_s, pre, gall, acc, slots, slot_rep, pack, place, a2a_s, a2a_r,
    in_sem, near_sem, ex_sem, rs_sem, rr_sem, tr_sem, agr_sem, agl_sem, gr_sem, gl_sem, gf_sem, gp_sem, sl_sem, slr_sem, as_sem, ar_sem,
):
    d = lax.axis_index("dp")
    m = lax.axis_index("mp")
    x, z = lax.div(d, NZ), lax.rem(d, NZ)
    y, c = lax.div(m, 2), lax.rem(m, 2)
    oc = 1 - c
    beta = lax.rem(2 * y - x + NX, NX)
    stays = (x == y).astype(I32)

    def q_copy(i, b):
        h = oc if i == 0 else c
        rows = pl.ds(pl.multiple_of(b * 256 + h * 128, 128), 128)
        return pltpu.make_async_copy(query_ref.at[rows], q_v.at[i, b], in_sem.at[i * 4 + b])

    def h_copy(k):
        return pltpu.make_async_copy(hess_ref.at[:, pl.ds(k * CW, CW)], h_v.at[k], in_sem.at[8 + k])

    def g_copy(i):
        return pltpu.make_async_copy(grads_ref.at[:, pl.ds(i * 1024, 1024)], g_v.at[i], in_sem.at[10 + i])

    h_copy(0).start()
    for b in range(4):
        q_copy(0, b).start()
    for b in range(4):
        q_copy(1, b).start()
    h_copy(1).start()
    small = [
        pltpu.make_async_copy(scale_ref, scale_v, in_sem.at[12]),
        pltpu.make_async_copy(member_hbm, member_ref, in_sem.at[13]),
        pltpu.make_async_copy(slot_hbm, slot_ref, in_sem.at[14]),
    ]
    for copy in small:
        copy.start()
    g_copy(0).start()
    g_copy(1).start()

    barrier = pltpu.get_barrier_semaphore()

    def greet(sem, targets):
        for target in targets:
            pl.semaphore_signal(sem, inc=1, device_id=target, device_id_type=MESH)

    line_x = [dev(x + o, y, z, c) for o in (2, 1, 3)]
    line_y = [dev(x, y + o, z, c) for o in (2, 1, 3)]
    line_z = [dev(x, y, z + o, c) for o in (4, 3, 5, 2, 6, 1, 7)]
    greet(barrier, line_z + line_y + line_x + [dev(x, y, z, oc)])

    def owner_of(o):
        return dev(lax.div(o, NZ), beta, lax.rem(o, NZ), c)

    def source_of(s):
        ys, zs = lax.div(s, NZ), lax.rem(s, NZ)
        return dev(2 * ys - y + NX, ys, zs, c)

    own_src = y * NZ + z
    me_owner = jnp.where(stays == 1, d, -1)
    me_source = jnp.where(stays == 1, own_src, -1)

    def partial(i, k):
        return jnp.dot(q_v[i].reshape(512, 2048), h_v[k], preferred_element_type=F32)

    def ex_copy(k):
        return pltpu.make_async_remote_copy(
            src_ref=ex_s.at[k], dst_ref=ex_r.at[k], send_sem=ex_sem.at[0, k], recv_sem=ex_sem.at[1, k],
            device_id=dev(x, y, z, oc), device_id_type=MESH)

    h_copy(0).wait()
    for b in range(4):
        q_copy(0, b).wait()
    ex_s[0] = partial(0, 0).astype(BF16).reshape(4, 128, CW)
    pl.semaphore_wait(barrier, 14)
    greet(near_sem.at[0], line_x)
    ex_copy(0).start()
    for b in range(4):
        q_copy(1, b).wait()
    own[0] = partial(1, 0).reshape(4, 128, CW)
    h_copy(1).wait()
    ex_s[1] = partial(0, 1).astype(BF16).reshape(4, 128, CW)
    ex_copy(1).start()

    def rs_copy(k, o):
        b = lax.rem(y + o, NY)
        return pltpu.make_async_remote_copy(
            src_ref=rs_s.at[k, b], dst_ref=rs_r.at[k, y], send_sem=rs_sem.at[k, o], recv_sem=rr_sem.at[k, y],
            device_id=dev(x, y + o, z, c), device_id_type=MESH)

    def rs_wait_recv(k, o):
        s = lax.rem(y + o, NY)
        pltpu.make_async_remote_copy(
            src_ref=rs_s.at[k, s], dst_ref=rs_r.at[k, s], send_sem=rs_sem.at[k, o], recv_sem=rr_sem.at[k, s],
            device_id=dev(x, y + o, z, c), device_id_type=MESH).wait_recv()

    def rs_send(k):
        ex_copy(k).wait_recv()
        for o in (2, 1, 3):
            b = lax.rem(y + o, NY)
            rs_s[k, b] = (own[k, b] + ex_r[k, b].astype(F32)).astype(BF16)
            rs_copy(k, o).start()

    rs_send(0)
    own[1] = partial(1, 1).reshape(4, 128, CW)
    rs_send(1)

    for copy in small:
        copy.wait()
    sct_ref[...] = jnp.transpose(scale_v[...])
    onehot = (lax.broadcasted_iota(I32, (128, 1024), 0) == member_ref[...]).astype(F32).astype(BF16)

    def group_half(h):
        g_copy(h).wait()
        for i in range(2):
            for k in range(KCH):
                col = (i * KCH + k) * CW
                parts = []
                for j in range(2):
                    at = col + j * 128
                    blk = (h * 1024 + at) // 128
                    parts.append((g_v[h, :, at : at + 128].astype(F32) * sct_ref[:, blk : blk + 1]).astype(BF16))
                deq = jnp.concatenate(parts, axis=1)
                gall[x, 4 * c + 2 * h + i, k] = jnp.dot(onehot, deq, preferred_element_type=F32).astype(BF16)

    def piece(xx, cc, h):
        return gall.at[lax.rem(xx, NX), pl.ds(4 * cc + 2 * h, 2)]

    def g_right(h):
        return pltpu.make_async_remote_copy(
            src_ref=piece(x, c, h), dst_ref=piece(x, c, h), send_sem=gr_sem.at[0, h], recv_sem=gr_sem.at[1, h],
            device_id=dev(x + 1, y, z, c), device_id_type=MESH)

    def g_left(h):
        return pltpu.make_async_remote_copy(
            src_ref=piece(x, c, h), dst_ref=piece(x, c, h), send_sem=gl_sem.at[0, h], recv_sem=gl_sem.at[1, h],
            device_id=dev(x + 3, y, z, c), device_id_type=MESH)

    def g_forward(h):
        src = piece(x + 3, c, 0) if h == 0 else piece(x + 1, c, 1)
        to = dev(x + 1, y, z, c) if h == 0 else dev(x + 3, y, z, c)
        return pltpu.make_async_remote_copy(
            src_ref=src, dst_ref=src, send_sem=gf_sem.at[0, h], recv_sem=gf_sem.at[1, h], device_id=to, device_id_type=MESH)

    def g_partner(o, h):
        return pltpu.make_async_remote_copy(
            src_ref=piece(x + o, c, h), dst_ref=piece(x + o, c, h), send_sem=gp_sem.at[0, o, h], recv_sem=gp_sem.at[1, o, h],
            device_id=dev(x, y, z, oc), device_id_type=MESH)

    def g_send(h):
        g_right(h).start()
        g_left(h).start()
        g_partner(0, h).start()

    group_half(0)
    g_send(0)

    def tr_copy(k):
        return pltpu.make_async_remote_copy(
            src_ref=tr_s.at[k], dst_ref=pre.at[k, z], send_sem=tr_sem.at[0, k], recv_sem=tr_sem.at[1, k],
            device_id=dev(2 * x - y + NX, x, z, c), device_id_type=MESH)

    def tr_send(k):
        total = own[k, y] + ex_r[k, y].astype(F32)
        for o in (1, 3, 2):
            rs_wait_recv(k, o)
            total += rs_r[k, lax.rem(y + o, NY)].astype(F32)
        tr_s[k] = total.astype(BF16)

        @pl.when(stays == 0)
        def _():
            tr_copy(k).start()

        @pl.when(stays == 1)
        def _():
            pre[k, z] = total.astype(BF16)

    pl.semaphore_wait(near_sem.at[0], 3)
    greet(near_sem.at[1], line_z)
    tr_send(0)
    group_half(1)
    tr_send(1)
    g_send(1)

    def slot_copy(s):
        return pltpu.make_async_remote_copy(
            src_ref=slot_ref, dst_ref=slots.at[d], send_sem=sl_sem.at[s], recv_sem=slr_sem.at[d],
            device_id=source_of(s), device_id_type=MESH)

    def slot_send(s, carry):
        @pl.when(s != me_source)
        def _():
            slot_copy(s).start()

        return carry

    pl.semaphore_wait(near_sem.at[1], 7)
    lax.fori_loop(0, 32, slot_send, 0)

    @pl.when(stays == 1)
    def _():
        slots[d] = slot_ref[...]

    def ag_copy(k, s, right):
        sems = agr_sem if right else agl_sem
        blk = lax.rem(z - s + NZ, NZ) if right else lax.rem(z + s, NZ)
        return pltpu.make_async_remote_copy(
            src_ref=pre.at[k, blk], dst_ref=pre.at[k, blk], send_sem=sems.at[0, k, s], recv_sem=sems.at[1, k, s],
            device_id=dev(x, y, z + (1 if right else NZ - 1), c), device_id_type=MESH)

    def ag_wait_recv(k, s, right):
        sems = agr_sem if right else agl_sem
        blk = lax.rem(z - s - 1 + NZ, NZ) if right else lax.rem(z + s + 1, NZ)
        pltpu.make_async_remote_copy(
            src_ref=pre.at[k, blk], dst_ref=pre.at[k, blk], send_sem=sems.at[0, k, s], recv_sem=sems.at[1, k, s],
            device_id=dev(x, y, z + (1 if right else NZ - 1), c), device_id_type=MESH).wait_recv()

    def steps(k, right):
        return 4 if (k == 0) == right else 3

    for k in range(KCH):
        @pl.when(stays == 0)
        def _():
            tr_copy(k).wait_recv()

        ag_copy(k, 0, True).start()
        ag_copy(k, 0, False).start()

    def ag_step(s):
        for k in range(KCH):
            for right in (True, False):
                if s < steps(k, right):
                    ag_wait_recv(k, s, right)
                    if s + 1 < steps(k, right):
                        ag_copy(k, s + 1, right).start()

    def g_wait(kind, h):
        src = {"r": (gr_sem, piece(x + 3, c, h)), "l": (gl_sem, piece(x + 1, c, h)), "f": (gf_sem, piece(x + 2, c, h))}
        sems, ref = src[kind]
        pltpu.make_async_remote_copy(
            src_ref=ref, dst_ref=ref, send_sem=sems.at[0, h], recv_sem=sems.at[1, h],
            device_id=dev(x + 1, y, z, c), device_id_type=MESH).wait_recv()

    def gp_wait(o, h):
        ref = piece(x + o, oc, h)
        pltpu.make_async_remote_copy(
            src_ref=ref, dst_ref=ref, send_sem=gp_sem.at[0, o, h], recv_sem=gp_sem.at[1, o, h],
            device_id=dev(x, y, z, oc), device_id_type=MESH).wait_recv()

    g_wait("r", 0)
    g_forward(0).start()
    g_partner(3, 0).start()
    g_wait("l", 0)
    g_partner(1, 0).start()
    ag_step(0)

    upper = (lax.broadcasted_iota(I32, (128, 128), 0) < lax.broadcasted_iota(I32, (128, 128), 1)).astype(F32).astype(BF16)

    def slot_wait(o, carry):
        @pl.when(o != me_owner)
        def _():
            pltpu.make_async_remote_copy(
                src_ref=slot_ref, dst_ref=slots.at[o], send_sem=sl_sem.at[o], recv_sem=slr_sem.at[o],
                device_id=source_of(o), device_id_type=MESH).wait_recv()

        return carry

    lax.fori_loop(0, 32, slot_wait, 0)
    row = lax.broadcasted_iota(I32, (1024, 128), 0)
    for xx in range(NX):
        hit = lax.shift_right_logical(slots[xx * NZ + z], 7) == lax.shift_right_logical(row, 5)
        mine = hit & ((lax.shift_right_logical(row, 3) & 3) == xx)
        rank = jnp.dot(hit.astype(F32).astype(BF16), upper, preferred_element_type=F32)
        pack[:, xx * 128 : (xx + 1) * 128] = jnp.where(
            mine & (rank == (row & 7).astype(F32)), 1.0, 0.0).astype(BF16)
    for j in range(32):
        slot_rep[j * 8 : (j + 1) * 8, :] = jnp.broadcast_to(slots[(j % 4) * NZ + j // 4], (8, 128))
    rep = slot_rep[...]
    row = lax.broadcasted_iota(I32, (256, 128), 0)
    hit = lax.shift_right_logical(rep, 7) == d
    rank = jnp.dot(hit.astype(F32).astype(BF16), upper, preferred_element_type=F32)
    taken = jnp.where(hit & (rank == (row & 7).astype(F32)), (rep & 127).astype(F32) + 1.0, 0.0)
    target = jnp.sum(taken, axis=1, keepdims=True) - 1.0
    place[...] = jnp.where(
        target == lax.broadcasted_iota(I32, (256, 128), 1).astype(F32), 1.0, 0.0).astype(BF16)

    ag_step(1)
    g_wait("l", 1)
    g_forward(1).start()
    g_partner(1, 1).start()
    g_wait("r", 1)
    g_partner(3, 1).start()
    ag_step(2)
    g_wait("f", 0)
    g_partner(2, 0).start()
    ag_step(3)

    def multiply(o):
        xx = lax.rem(x + o, NX)

        def body(zz, total):
            for k in range(KCH):
                total += lax.dot_general(
                    gall[xx, zz, k], pre[k, zz], (((1,), (1,)), ((), ())), preferred_element_type=F32)
            return total

        acc[xx] = lax.fori_loop(0, NZ, body, jnp.zeros((128, 128), F32))

    for o in (0, 1, 3):
        gp_wait(o, 0)
        gp_wait(o, 1)
        multiply(o)
    g_wait("f", 1)
    g_partner(2, 1).start()
    gp_wait(2, 0)
    gp_wait(2, 1)
    multiply(2)

    a2a_s[...] = jnp.dot(
        pack[...], acc[...].reshape(512, 128).astype(BF16), preferred_element_type=F32).astype(BF16).reshape(32, 32, 128)

    def out_copy(o):
        return pltpu.make_async_remote_copy(
            src_ref=a2a_s.at[o], dst_ref=a2a_r.at[own_src], send_sem=as_sem.at[o], recv_sem=ar_sem.at[own_src],
            device_id=owner_of(o), device_id_type=MESH)

    def out_send(i, carry):
        o = lax.rem(d + i, 32)

        @pl.when(o != me_owner)
        def _():
            out_copy(o).start()

        return carry

    lax.fori_loop(0, 32, out_send, 0)

    @pl.when(stays == 1)
    def _():
        a2a_r[own_src] = a2a_s[d]

    def out_wait(s, carry):
        @pl.when(s != me_source)
        def _():
            pltpu.make_async_remote_copy(
                src_ref=a2a_s.at[s], dst_ref=a2a_r.at[s], send_sem=as_sem.at[s], recv_sem=ar_sem.at[s],
                device_id=source_of(s), device_id_type=MESH).wait_recv()

        return carry

    lax.fori_loop(0, 32, out_wait, 0)
    total = jnp.zeros((128, 128), F32)
    for ys in range(NY):
        rows = a2a_r[ys * NZ : (ys + 1) * NZ].reshape(256, 128)
        total += lax.dot_general(place[...], rows, (((0,), (0,)), ((), ())), preferred_element_type=F32)
    out_ref[...] = total

    for k in range(KCH):
        ex_copy(k).wait_send()
        for o in (1, 2, 3):
            rs_copy(k, o).wait_send()

        @pl.when(stays == 0)
        def _():
            tr_copy(k).wait_send()

        for right in (True, False):
            for s in range(steps(k, right)):
                ag_copy(k, s, right).wait_send()
    for h in range(2):
        g_right(h).wait_send()
        g_left(h).wait_send()
        g_forward(h).wait_send()
        for o in range(NX):
            g_partner(o, h).wait_send()

    def drain(i, carry):
        @pl.when(i != me_source)
        def _():
            slot_copy(i).wait_send()

        @pl.when(i != me_owner)
        def _():
            out_copy(i).wait_send()

        return carry

    lax.fori_loop(0, 32, drain, 0)


def local(grads, scales, example_group, group_slot, inv_hess, queries):
    vmem = pl.BlockSpec(memory_space=pltpu.VMEM)
    hbm = pl.BlockSpec(memory_space=pltpu.HBM)
    dma = pltpu.SemaphoreType.DMA
    return pl.pallas_call(
        kernel,
        out_shape=jax.ShapeDtypeStruct((128, 128), F32),
        in_specs=[hbm] * 6,
        out_specs=vmem,
        scratch_shapes=[
            pltpu.VMEM((16, 1024), F32),
            pltpu.VMEM((1024, 16), F32),
            pltpu.VMEM((1, 1024), I32),
            pltpu.VMEM((1, 128), I32),
            pltpu.VMEM((2, 4, 128, 2048), BF16),
            pltpu.VMEM((KCH, 2048, CW), BF16),
            pltpu.VMEM((2, 1024, 1024), BF16),
            pltpu.VMEM((KCH, 4, 128, CW), BF16),
            pltpu.VMEM((KCH, 4, 128, CW), BF16),
            pltpu.VMEM((KCH, 4, 128, CW), F32),
            pltpu.VMEM((KCH, 4, 128, CW), BF16),
            pltpu.VMEM((KCH, 4, 128, CW), BF16),
            pltpu.VMEM((KCH, 128, CW), BF16),
            pltpu.VMEM((KCH, NZ, 128, CW), BF16),
            pltpu.VMEM((NX, NZ, KCH, 128, CW), BF16),
            pltpu.VMEM((NX, 128, 128), F32),
            pltpu.VMEM((32, 1, 128), I32),
            pltpu.VMEM((256, 128), I32),
            pltpu.VMEM((1024, 512), BF16),
            pltpu.VMEM((256, 128), BF16),
            pltpu.VMEM((32, 32, 128), BF16),
            pltpu.VMEM((32, 32, 128), BF16),
            dma((15,)),
            pltpu.SemaphoreType.REGULAR((2,)),
            dma((2, KCH)),
            dma((KCH, 4)),
            dma((KCH, 4)),
            dma((2, KCH)),
            dma((2, KCH, 4)),
            dma((2, KCH, 4)),
            dma((2, 2)),
            dma((2, 2)),
            dma((2, 2)),
            dma((2, 4, 2)),
            dma((32,)),
            dma((32,)),
            dma((32,)),
            dma((32,)),
        ],
        compiler_params=pltpu.CompilerParams(collective_id=0, has_side_effects=True, vmem_limit_bytes=67_043_328),
        name="scores",
    )(grads, scales, example_group, group_slot.reshape(1, 128), inv_hess, queries)


def solution(mesh):
    in_specs = (P("dp", "mp"), P("mp", "dp"), P("dp", None), P("dp"), P("mp", "dp"), P(None, "mp"))
    out_specs = P("dp", "mp")
    return jax.shard_map(local, mesh=mesh, in_specs=in_specs, out_specs=out_specs, check_vma=False)
```

```python
import functools

import jax
import jax.numpy as jnp
from jax import lax
from jax.experimental import pallas as pl
from jax.experimental.pallas import tpu as pltpu
from jax.sharding import PartitionSpec as P

MESH = pl.DeviceIdType.MESH
BF16, F32, I32 = jnp.bfloat16, jnp.float32, jnp.int32
NX, NY, NZ = 4, 4, 8
KCH = 2
CW = 256


def dev(x, y, z, c):
    return (lax.rem(x, NX) * NZ + lax.rem(z, NZ), lax.rem(y, NY) * 2 + c)


def kernel(
    grads_ref, scale_ref, member_hbm, slot_hbm, hess_ref, query_ref, out_ref,
    scale_v, sct_ref, member_ref, slot_ref, q_v, h_v, g_v, ex_s, ex_r, own, rs_s, rs_r, tr_s, pre, gall, acc, slots, slot_rep, pack, place, a2a_s, a2a_r,
    in_sem, near_sem, ex_sem, rs_sem, rr_sem, tr_sem, agr_sem, agl_sem, gr_sem, gl_sem, gf_sem, gp_sem, sl_sem, slr_sem, as_sem, ar_sem,
):
    d = lax.axis_index("dp")
    m = lax.axis_index("mp")
    x, z = lax.div(d, NZ), lax.rem(d, NZ)
    y, c = lax.div(m, 2), lax.rem(m, 2)
    oc = 1 - c
    beta = lax.rem(2 * y - x + NX, NX)
    stays = (x == y).astype(I32)

    def q_copy(i, b):
        h = oc if i == 0 else c
        rows = pl.ds(pl.multiple_of(b * 256 + h * 128, 128), 128)
        return pltpu.make_async_copy(query_ref.at[rows], q_v.at[i, b], in_sem.at[i * 4 + b])

    def h_copy(k):
        return pltpu.make_async_copy(hess_ref.at[:, pl.ds(k * CW, CW)], h_v.at[k], in_sem.at[8 + k])

    def g_copy(i):
        return pltpu.make_async_copy(grads_ref.at[:, pl.ds(i * 1024, 1024)], g_v.at[i], in_sem.at[10 + i])

    h_copy(0).start()
    for b in range(4):
        q_copy(0, b).start()
    for b in range(4):
        q_copy(1, b).start()
    h_copy(1).start()
    small = [
        pltpu.make_async_copy(scale_ref, scale_v, in_sem.at[12]),
        pltpu.make_async_copy(member_hbm, member_ref, in_sem.at[13]),
        pltpu.make_async_copy(slot_hbm, slot_ref, in_sem.at[14]),
    ]
    for copy in small:
        copy.start()
    g_copy(0).start()
    g_copy(1).start()

    barrier = pltpu.get_barrier_semaphore()

    def greet(sem, targets):
        for target in targets:
            pl.semaphore_signal(sem, inc=1, device_id=target, device_id_type=MESH)

    line_x = [dev(x + o, y, z, c) for o in (2, 1, 3)]
    line_y = [dev(x, y + o, z, c) for o in (2, 1, 3)]
    line_z = [dev(x, y, z + o, c) for o in (4, 3, 5, 2, 6, 1, 7)]
    greet(barrier, line_z + line_y + line_x + [dev(x, y, z, oc)])

    def owner_of(o):
        return dev(lax.div(o, NZ), beta, lax.rem(o, NZ), c)

    def source_of(s):
        ys, zs = lax.div(s, NZ), lax.rem(s, NZ)
        return dev(2 * ys - y + NX, ys, zs, c)

    own_src = y * NZ + z
    me_owner = jnp.where(stays == 1, d, -1)
    me_source = jnp.where(stays == 1, own_src, -1)

    def partial(i, k):
        return jnp.dot(q_v[i].reshape(512, 2048), h_v[k], preferred_element_type=F32)

    def ex_copy(k):
        return pltpu.make_async_remote_copy(
            src_ref=ex_s.at[k], dst_ref=ex_r.at[k], send_sem=ex_sem.at[0, k], recv_sem=ex_sem.at[1, k],
            device_id=dev(x, y, z, oc), device_id_type=MESH)

    h_copy(0).wait()
    for b in range(4):
        q_copy(0, b).wait()
    ex_s[0] = partial(0, 0).astype(BF16).reshape(4, 128, CW)
    pl.semaphore_wait(barrier, 14)
    greet(near_sem.at[0], line_x)
    ex_copy(0).start()
    for b in range(4):
        q_copy(1, b).wait()
    own[0] = partial(1, 0).reshape(4, 128, CW)
    h_copy(1).wait()
    ex_s[1] = partial(0, 1).astype(BF16).reshape(4, 128, CW)
    ex_copy(1).start()

    def rs_copy(k, o):
        b = lax.rem(y + o, NY)
        return pltpu.make_async_remote_copy(
            src_ref=rs_s.at[k, b], dst_ref=rs_r.at[k, y], send_sem=rs_sem.at[k, o], recv_sem=rr_sem.at[k, y],
            device_id=dev(x, y + o, z, c), device_id_type=MESH)

    def rs_wait_recv(k, o):
        s = lax.rem(y + o, NY)
        pltpu.make_async_remote_copy(
            src_ref=rs_s.at[k, s], dst_ref=rs_r.at[k, s], send_sem=rs_sem.at[k, o], recv_sem=rr_sem.at[k, s],
            device_id=dev(x, y + o, z, c), device_id_type=MESH).wait_recv()

    def rs_send(k):
        ex_copy(k).wait_recv()
        for o in (2, 1, 3):
            b = lax.rem(y + o, NY)
            rs_s[k, b] = (own[k, b] + ex_r[k, b].astype(F32)).astype(BF16)
            rs_copy(k, o).start()

    rs_send(0)
    own[1] = partial(1, 1).reshape(4, 128, CW)
    rs_send(1)

    for copy in small:
        copy.wait()
    sct_ref[...] = jnp.transpose(scale_v[...])
    onehot = (lax.broadcasted_iota(I32, (128, 1024), 0) == member_ref[...]).astype(F32).astype(BF16)

    def group_half(h):
        g_copy(h).wait()
        for i in range(2):
            for k in range(KCH):
                col = (i * KCH + k) * CW
                parts = []
                for j in range(2):
                    at = col + j * 128
                    blk = (h * 1024 + at) // 128
                    parts.append((g_v[h, :, at : at + 128].astype(F32) * sct_ref[:, blk : blk + 1]).astype(BF16))
                deq = jnp.concatenate(parts, axis=1)
                gall[x, 4 * c + 2 * h + i, k] = jnp.dot(onehot, deq, preferred_element_type=F32).astype(BF16)

    def piece(xx, cc, h):
        return gall.at[lax.rem(xx, NX), 4 * cc + h]

    def g_right(h):
        return pltpu.make_async_remote_copy(
            src_ref=piece(x, c, h), dst_ref=piece(x, c, h), send_sem=gr_sem.at[0, h], recv_sem=gr_sem.at[1, h],
            device_id=dev(x + 1, y, z, c), device_id_type=MESH)

    def g_left(h):
        return pltpu.make_async_remote_copy(
            src_ref=piece(x, c, h), dst_ref=piece(x, c, h), send_sem=gl_sem.at[0, h], recv_sem=gl_sem.at[1, h],
            device_id=dev(x + 3, y, z, c), device_id_type=MESH)

    def g_forward(h):
        src = piece(x + 3, c, h) if h < 2 else piece(x + 1, c, h)
        to = dev(x + 1, y, z, c) if h < 2 else dev(x + 3, y, z, c)
        return pltpu.make_async_remote_copy(
            src_ref=src, dst_ref=src, send_sem=gf_sem.at[0, h], recv_sem=gf_sem.at[1, h], device_id=to, device_id_type=MESH)

    def g_partner(o, h):
        return pltpu.make_async_remote_copy(
            src_ref=piece(x + o, c, h), dst_ref=piece(x + o, c, h), send_sem=gp_sem.at[0, o, h], recv_sem=gp_sem.at[1, o, h],
            device_id=dev(x, y, z, oc), device_id_type=MESH)

    def g_send(h):
        g_right(h).start()
        g_left(h).start()
        g_partner(0, h).start()

    group_half(0)
    g_send(0)
    group_half(1)

    def tr_copy(k):
        return pltpu.make_async_remote_copy(
            src_ref=tr_s.at[k], dst_ref=pre.at[k, z], send_sem=tr_sem.at[0, k], recv_sem=tr_sem.at[1, k],
            device_id=dev(2 * x - y + NX, x, z, c), device_id_type=MESH)

    def tr_send(k):
        total = own[k, y] + ex_r[k, y].astype(F32)
        for o in (1, 3, 2):
            rs_wait_recv(k, o)
            total += rs_r[k, lax.rem(y + o, NY)].astype(F32)
        tr_s[k] = total.astype(BF16)

        @pl.when(stays == 0)
        def _():
            tr_copy(k).start()

        @pl.when(stays == 1)
        def _():
            pre[k, z] = total.astype(BF16)

    pl.semaphore_wait(near_sem.at[0], 3)
    greet(near_sem.at[1], line_z)
    tr_send(0)
    tr_send(1)
    for h in (1, 2, 3):
        g_send(h)

    def ag_copy(k, s, right):
        sems = agr_sem if right else agl_sem
        blk = lax.rem(z - s + NZ, NZ) if right else lax.rem(z + s, NZ)
        return pltpu.make_async_remote_copy(
            src_ref=pre.at[k, blk], dst_ref=pre.at[k, blk], send_sem=sems.at[0, k, s], recv_sem=sems.at[1, k, s],
            device_id=dev(x, y, z + (1 if right else NZ - 1), c), device_id_type=MESH)

    def ag_wait_recv(k, s, right):
        sems = agr_sem if right else agl_sem
        blk = lax.rem(z - s - 1 + NZ, NZ) if right else lax.rem(z + s + 1, NZ)
        pltpu.make_async_remote_copy(
            src_ref=pre.at[k, blk], dst_ref=pre.at[k, blk], send_sem=sems.at[0, k, s], recv_sem=sems.at[1, k, s],
            device_id=dev(x, y, z + (1 if right else NZ - 1), c), device_id_type=MESH).wait_recv()

    def steps(k, right):
        return 4 if (k == 0) == right else 3

    for k in range(KCH):
        @pl.when(stays == 0)
        def _():
            tr_copy(k).wait_recv()

        ag_copy(k, 0, True).start()
        ag_copy(k, 0, False).start()

    def slot_copy(s):
        return pltpu.make_async_remote_copy(
            src_ref=slot_ref, dst_ref=slots.at[d], send_sem=sl_sem.at[s], recv_sem=slr_sem.at[d],
            device_id=source_of(s), device_id_type=MESH)

    def slot_send(s, carry):
        @pl.when(s != me_source)
        def _():
            slot_copy(s).start()

        return carry

    pl.semaphore_wait(near_sem.at[1], 7)
    lax.fori_loop(0, 32, slot_send, 0)

    @pl.when(stays == 1)
    def _():
        slots[d] = slot_ref[...]

    def ag_step(s):
        for k in range(KCH):
            for right in (True, False):
                if s < steps(k, right):
                    ag_wait_recv(k, s, right)
                    if s + 1 < steps(k, right):
                        ag_copy(k, s + 1, right).start()

    def g_wait(kind, h):
        src = {"r": (gr_sem, piece(x + 3, c, h)), "l": (gl_sem, piece(x + 1, c, h)), "f": (gf_sem, piece(x + 2, c, h))}
        sems, ref = src[kind]
        pltpu.make_async_remote_copy(
            src_ref=ref, dst_ref=ref, send_sem=sems.at[0, h], recv_sem=sems.at[1, h],
            device_id=dev(x + 1, y, z, c), device_id_type=MESH).wait_recv()

    def gp_wait(o, h):
        ref = piece(x + o, oc, h)
        pltpu.make_async_remote_copy(
            src_ref=ref, dst_ref=ref, send_sem=gp_sem.at[0, o, h], recv_sem=gp_sem.at[1, o, h],
            device_id=dev(x, y, z, oc), device_id_type=MESH).wait_recv()

    def g_near(h):
        g_wait("r", h)
        if h < 2:
            g_forward(h).start()
        g_partner(3, h).start()
        g_wait("l", h)
        if h >= 2:
            g_forward(h).start()
        g_partner(1, h).start()

    def g_far(h):
        g_wait("f", h)
        g_partner(2, h).start()

    def multiply(others, blocks, fresh):
        rows = [lax.rem(x + o, NX) for o in others]
        left = jnp.concatenate(
            [jnp.concatenate([gall[xx, zz, k] for zz in blocks for k in range(KCH)], axis=1) for xx in rows], axis=0)
        right = jnp.concatenate([pre[k, zz] for zz in blocks for k in range(KCH)], axis=1)
        part = lax.dot_general(left, right, (((1,), (1,)), ((), ())), preferred_element_type=F32)
        for i, xx in enumerate(rows):
            piece_of = part[i * 128 : (i + 1) * 128]
            acc[xx] = piece_of if fresh else acc[xx] + piece_of

    def away(*steps):
        return [lax.rem(z + r, NZ) for r in steps]

    g_near(0)
    g_near(1)
    ag_step(0)
    g_near(2)
    ag_step(1)
    g_near(3)
    ag_step(2)
    for o in (0, 1, 3):
        for h in range(4):
            gp_wait(o, h)
    multiply((0, 1, 3), away(0, 1, 7), True)
    multiply((0, 1, 3), away(2, 6), False)
    multiply((0, 1, 3), away(3, 5), False)
    g_far(0)
    g_far(2)
    upper = (lax.broadcasted_iota(I32, (128, 128), 0) < lax.broadcasted_iota(I32, (128, 128), 1)).astype(F32).astype(BF16)

    def slot_wait(o, carry):
        @pl.when(o != me_owner)
        def _():
            pltpu.make_async_remote_copy(
                src_ref=slot_ref, dst_ref=slots.at[o], send_sem=sl_sem.at[o], recv_sem=slr_sem.at[o],
                device_id=source_of(o), device_id_type=MESH).wait_recv()

        return carry

    lax.fori_loop(0, 32, slot_wait, 0)
    row = lax.broadcasted_iota(I32, (1024, 128), 0)
    for xx in range(NX):
        hit = lax.shift_right_logical(slots[xx * NZ + z], 7) == lax.shift_right_logical(row, 5)
        mine = hit & ((lax.shift_right_logical(row, 3) & 3) == xx)
        rank = jnp.dot(hit.astype(F32).astype(BF16), upper, preferred_element_type=F32)
        pack[:, xx * 128 : (xx + 1) * 128] = jnp.where(
            mine & (rank == (row & 7).astype(F32)), 1.0, 0.0).astype(BF16)
    for j in range(32):
        slot_rep[j * 8 : (j + 1) * 8, :] = jnp.broadcast_to(slots[(j % 4) * NZ + j // 4], (8, 128))
    rep = slot_rep[...]
    row = lax.broadcasted_iota(I32, (256, 128), 0)
    hit = lax.shift_right_logical(rep, 7) == d
    rank = jnp.dot(hit.astype(F32).astype(BF16), upper, preferred_element_type=F32)
    taken = jnp.where(hit & (rank == (row & 7).astype(F32)), (rep & 127).astype(F32) + 1.0, 0.0)
    target = jnp.sum(taken, axis=1, keepdims=True) - 1.0
    place[...] = jnp.where(
        target == lax.broadcasted_iota(I32, (256, 128), 1).astype(F32), 1.0, 0.0).astype(BF16)

    ag_step(3)
    multiply((0, 1, 3), away(4), False)
    for i, h in enumerate((0, 2)):
        gp_wait(2, h)
        multiply((2,), (h, 4 + h), i == 0)
    g_far(1)
    g_far(3)
    for h in (1, 3):
        gp_wait(2, h)
        multiply((2,), (h, 4 + h), False)

    a2a_s[...] = jnp.dot(
        pack[...], acc[...].reshape(512, 128).astype(BF16), preferred_element_type=F32).astype(BF16).reshape(32, 32, 128)

    def out_copy(o):
        return pltpu.make_async_remote_copy(
            src_ref=a2a_s.at[o], dst_ref=a2a_r.at[own_src], send_sem=as_sem.at[o], recv_sem=ar_sem.at[own_src],
            device_id=owner_of(o), device_id_type=MESH)

    def out_send(i, carry):
        jx, jz = lax.div(i, NZ), lax.rem(i, NZ)
        ox = lax.rem(x + 2 + lax.div(jx + 1, 2) * (1 - 2 * lax.rem(jx, 2)), NX)
        oz = lax.rem(z + 4 + lax.div(jz + 1, 2) * (1 - 2 * lax.rem(jz, 2)), NZ)
        o = ox * NZ + oz

        @pl.when(o != me_owner)
        def _():
            out_copy(o).start()

        return carry

    lax.fori_loop(0, 32, out_send, 0)

    @pl.when(stays == 1)
    def _():
        a2a_r[own_src] = a2a_s[d]

    def out_wait(s, carry):
        @pl.when(s != me_source)
        def _():
            pltpu.make_async_remote_copy(
                src_ref=a2a_s.at[s], dst_ref=a2a_r.at[s], send_sem=as_sem.at[s], recv_sem=ar_sem.at[s],
                device_id=source_of(s), device_id_type=MESH).wait_recv()

        return carry

    lax.fori_loop(0, 32, out_wait, 0)
    total = jnp.zeros((128, 128), F32)
    for ys in range(NY):
        rows = a2a_r[ys * NZ : (ys + 1) * NZ].reshape(256, 128)
        total += lax.dot_general(place[...], rows, (((0,), (0,)), ((), ())), preferred_element_type=F32)
    out_ref[...] = total

    for k in range(KCH):
        ex_copy(k).wait_send()
        for o in (1, 2, 3):
            rs_copy(k, o).wait_send()

        @pl.when(stays == 0)
        def _():
            tr_copy(k).wait_send()

        for right in (True, False):
            for s in range(steps(k, right)):
                ag_copy(k, s, right).wait_send()
    for h in range(4):
        g_right(h).wait_send()
        g_left(h).wait_send()
        g_forward(h).wait_send()
        for o in range(NX):
            g_partner(o, h).wait_send()

    def drain(i, carry):
        @pl.when(i != me_source)
        def _():
            slot_copy(i).wait_send()

        @pl.when(i != me_owner)
        def _():
            out_copy(i).wait_send()

        return carry

    lax.fori_loop(0, 32, drain, 0)


def local(grads, scales, example_group, group_slot, inv_hess, queries):
    vmem = pl.BlockSpec(memory_space=pltpu.VMEM)
    hbm = pl.BlockSpec(memory_space=pltpu.HBM)
    dma = pltpu.SemaphoreType.DMA
    return pl.pallas_call(
        kernel,
        out_shape=jax.ShapeDtypeStruct((128, 128), F32),
        in_specs=[hbm] * 6,
        out_specs=vmem,
        scratch_shapes=[
            pltpu.VMEM((16, 1024), F32),
            pltpu.VMEM((1024, 16), F32),
            pltpu.VMEM((1, 1024), I32),
            pltpu.VMEM((1, 128), I32),
            pltpu.VMEM((2, 4, 128, 2048), BF16),
            pltpu.VMEM((KCH, 2048, CW), BF16),
            pltpu.VMEM((2, 1024, 1024), BF16),
            pltpu.VMEM((KCH, 4, 128, CW), BF16),
            pltpu.VMEM((KCH, 4, 128, CW), BF16),
            pltpu.VMEM((KCH, 4, 128, CW), F32),
            pltpu.VMEM((KCH, 4, 128, CW), BF16),
            pltpu.VMEM((KCH, 4, 128, CW), BF16),
            pltpu.VMEM((KCH, 128, CW), BF16),
            pltpu.VMEM((KCH, NZ, 128, CW), BF16),
            pltpu.VMEM((NX, NZ, KCH, 128, CW), BF16),
            pltpu.VMEM((NX, 128, 128), F32),
            pltpu.VMEM((32, 1, 128), I32),
            pltpu.VMEM((256, 128), I32),
            pltpu.VMEM((1024, 512), BF16),
            pltpu.VMEM((256, 128), BF16),
            pltpu.VMEM((32, 32, 128), BF16),
            pltpu.VMEM((32, 32, 128), BF16),
            dma((15,)),
            pltpu.SemaphoreType.REGULAR((2,)),
            dma((2, KCH)),
            dma((KCH, 4)),
            dma((KCH, 4)),
            dma((2, KCH)),
            dma((2, KCH, 4)),
            dma((2, KCH, 4)),
            dma((2, 4)),
            dma((2, 4)),
            dma((2, 4)),
            dma((2, 4, 4)),
            dma((32,)),
            dma((32,)),
            dma((32,)),
            dma((32,)),
        ],
        compiler_params=pltpu.CompilerParams(collective_id=0, has_side_effects=True, vmem_limit_bytes=67_043_328),
        name="scores",
    )(grads, scales, example_group, group_slot.reshape(1, 128), inv_hess, queries)


def solution(mesh):
    in_specs = (P("dp", "mp"), P("mp", "dp"), P("dp", None), P("dp"), P("mp", "dp"), P(None, "mp"))
    out_specs = P("dp", "mp")
    return jax.shard_map(local, mesh=mesh, in_specs=in_specs, out_specs=out_specs, check_vma=False)
```

```python
import functools

import jax
import jax.numpy as jnp
from jax import lax
from jax.experimental import pallas as pl
from jax.experimental.pallas import tpu as pltpu
from jax.sharding import PartitionSpec as P

MESH = pl.DeviceIdType.MESH
BF16, F32, I32 = jnp.bfloat16, jnp.float32, jnp.int32
NX, NY, NZ = 4, 4, 8
KCH = 2
CW = 256


def dev(x, y, z, c):
    return (lax.rem(x, NX) * NZ + lax.rem(z, NZ), lax.rem(y, NY) * 2 + c)


def kernel(
    grads_ref, scale_ref, member_hbm, slot_hbm, hess_ref, query_ref, out_ref,
    scale_v, sct_ref, member_ref, slot_ref, q_v, h_v, g_v, ex_s, ex_r, own, rs_s, rs_r, tr_s, pre, gall, acc, slots, slot_rep, pack, place, out_s, out_r, mid_s, mid_r,
    in_sem, near_sem, ex_sem, rs_sem, rr_sem, tr_sem, agr_sem, agl_sem, gr_sem, gl_sem, gf_sem, gp_sem, sl_sem, slr_sem, os_sem, or_sem, ms_sem, mr_sem,
):
    d = lax.axis_index("dp")
    m = lax.axis_index("mp")
    x, z = lax.div(d, NZ), lax.rem(d, NZ)
    y, c = lax.div(m, 2), lax.rem(m, 2)
    oc = 1 - c
    beta = lax.rem(2 * y - x + NX, NX)
    stays = (x == y).astype(I32)

    def q_copy(i, b):
        h = oc if i == 0 else c
        rows = pl.ds(pl.multiple_of(b * 256 + h * 128, 128), 128)
        return pltpu.make_async_copy(query_ref.at[rows], q_v.at[i, b], in_sem.at[i * 4 + b])

    def h_copy(k):
        return pltpu.make_async_copy(hess_ref.at[:, pl.ds(k * CW, CW)], h_v.at[k], in_sem.at[8 + k])

    def g_copy(i):
        return pltpu.make_async_copy(grads_ref.at[:, pl.ds(i * 1024, 1024)], g_v.at[i], in_sem.at[10 + i])

    h_copy(0).start()
    for b in range(4):
        q_copy(0, b).start()
    for b in range(4):
        q_copy(1, b).start()
    h_copy(1).start()
    small = [
        pltpu.make_async_copy(scale_ref, scale_v, in_sem.at[12]),
        pltpu.make_async_copy(member_hbm, member_ref, in_sem.at[13]),
        pltpu.make_async_copy(slot_hbm, slot_ref, in_sem.at[14]),
    ]
    for copy in small:
        copy.start()
    g_copy(0).start()
    g_copy(1).start()

    barrier = pltpu.get_barrier_semaphore()

    def greet(sem, targets):
        for target in targets:
            pl.semaphore_signal(sem, inc=1, device_id=target, device_id_type=MESH)

    line_x = [dev(x + o, y, z, c) for o in (2, 1, 3)]
    line_y = [dev(x, y + o, z, c) for o in (2, 1, 3)]
    line_z = [dev(x, y, z + o, c) for o in (4, 3, 5, 2, 6, 1, 7)]
    greet(barrier, line_z + line_y + line_x + [dev(x, y, z, oc)])

    def source_of(s):
        ys, zs = lax.div(s, NZ), lax.rem(s, NZ)
        return dev(2 * ys - y + NX, ys, zs, c)

    own_src = y * NZ + z
    me_owner = jnp.where(stays == 1, d, -1)
    me_source = jnp.where(stays == 1, own_src, -1)

    def partial(i, k):
        return jnp.dot(q_v[i].reshape(512, 2048), h_v[k], preferred_element_type=F32)

    def ex_copy(k):
        return pltpu.make_async_remote_copy(
            src_ref=ex_s.at[k], dst_ref=ex_r.at[k], send_sem=ex_sem.at[0, k], recv_sem=ex_sem.at[1, k],
            device_id=dev(x, y, z, oc), device_id_type=MESH)

    h_copy(0).wait()
    for b in range(4):
        q_copy(0, b).wait()
    ex_s[0] = partial(0, 0).astype(BF16).reshape(4, 128, CW)
    pl.semaphore_wait(barrier, 14)
    greet(near_sem.at[0], line_x)
    ex_copy(0).start()
    for b in range(4):
        q_copy(1, b).wait()
    own[0] = partial(1, 0).reshape(4, 128, CW)
    h_copy(1).wait()
    ex_s[1] = partial(0, 1).astype(BF16).reshape(4, 128, CW)
    ex_copy(1).start()

    def rs_copy(k, o):
        b = lax.rem(y + o, NY)
        return pltpu.make_async_remote_copy(
            src_ref=rs_s.at[k, b], dst_ref=rs_r.at[k, y], send_sem=rs_sem.at[k, o], recv_sem=rr_sem.at[k, y],
            device_id=dev(x, y + o, z, c), device_id_type=MESH)

    def rs_wait_recv(k, o):
        s = lax.rem(y + o, NY)
        pltpu.make_async_remote_copy(
            src_ref=rs_s.at[k, s], dst_ref=rs_r.at[k, s], send_sem=rs_sem.at[k, o], recv_sem=rr_sem.at[k, s],
            device_id=dev(x, y + o, z, c), device_id_type=MESH).wait_recv()

    def rs_send(k):
        ex_copy(k).wait_recv()
        for o in (2, 1, 3):
            b = lax.rem(y + o, NY)
            rs_s[k, b] = (own[k, b] + ex_r[k, b].astype(F32)).astype(BF16)
            rs_copy(k, o).start()

    rs_send(0)
    own[1] = partial(1, 1).reshape(4, 128, CW)
    rs_send(1)

    for copy in small:
        copy.wait()
    sct_ref[...] = jnp.transpose(scale_v[...])
    onehot = (lax.broadcasted_iota(I32, (128, 1024), 0) == member_ref[...]).astype(F32).astype(BF16)

    def group_half(h):
        g_copy(h).wait()
        for i in range(2):
            for k in range(KCH):
                col = (i * KCH + k) * CW
                parts = []
                for j in range(2):
                    at = col + j * 128
                    blk = (h * 1024 + at) // 128
                    parts.append((g_v[h, :, at : at + 128].astype(F32) * sct_ref[:, blk : blk + 1]).astype(BF16))
                deq = jnp.concatenate(parts, axis=1)
                gall[x, 4 * c + 2 * h + i, k] = jnp.dot(onehot, deq, preferred_element_type=F32).astype(BF16)

    def piece(xx, cc, h):
        return gall.at[lax.rem(xx, NX), 4 * cc + h]

    def g_right(h):
        return pltpu.make_async_remote_copy(
            src_ref=piece(x, c, h), dst_ref=piece(x, c, h), send_sem=gr_sem.at[0, h], recv_sem=gr_sem.at[1, h],
            device_id=dev(x + 1, y, z, c), device_id_type=MESH)

    def g_left(h):
        return pltpu.make_async_remote_copy(
            src_ref=piece(x, c, h), dst_ref=piece(x, c, h), send_sem=gl_sem.at[0, h], recv_sem=gl_sem.at[1, h],
            device_id=dev(x + 3, y, z, c), device_id_type=MESH)

    def g_forward(h):
        src = piece(x + 3, c, h) if h < 2 else piece(x + 1, c, h)
        to = dev(x + 1, y, z, c) if h < 2 else dev(x + 3, y, z, c)
        return pltpu.make_async_remote_copy(
            src_ref=src, dst_ref=src, send_sem=gf_sem.at[0, h], recv_sem=gf_sem.at[1, h], device_id=to, device_id_type=MESH)

    def g_partner(o, h):
        return pltpu.make_async_remote_copy(
            src_ref=piece(x + o, c, h), dst_ref=piece(x + o, c, h), send_sem=gp_sem.at[0, o, h], recv_sem=gp_sem.at[1, o, h],
            device_id=dev(x, y, z, oc), device_id_type=MESH)

    def g_send(h):
        g_right(h).start()
        g_left(h).start()
        g_partner(0, h).start()

    group_half(0)
    g_send(0)
    group_half(1)

    def tr_copy(k):
        return pltpu.make_async_remote_copy(
            src_ref=tr_s.at[k], dst_ref=pre.at[k, z], send_sem=tr_sem.at[0, k], recv_sem=tr_sem.at[1, k],
            device_id=dev(2 * x - y + NX, x, z, c), device_id_type=MESH)

    def tr_send(k):
        total = own[k, y] + ex_r[k, y].astype(F32)
        for o in (1, 3, 2):
            rs_wait_recv(k, o)
            total += rs_r[k, lax.rem(y + o, NY)].astype(F32)
        tr_s[k] = total.astype(BF16)

        @pl.when(stays == 0)
        def _():
            tr_copy(k).start()

        @pl.when(stays == 1)
        def _():
            pre[k, z] = total.astype(BF16)

    pl.semaphore_wait(near_sem.at[0], 3)
    greet(near_sem.at[1], line_z)
    tr_send(0)
    tr_send(1)
    for h in (1, 2, 3):
        g_send(h)

    def ag_copy(k, s, right):
        sems = agr_sem if right else agl_sem
        blk = lax.rem(z - s + NZ, NZ) if right else lax.rem(z + s, NZ)
        return pltpu.make_async_remote_copy(
            src_ref=pre.at[k, blk], dst_ref=pre.at[k, blk], send_sem=sems.at[0, k, s], recv_sem=sems.at[1, k, s],
            device_id=dev(x, y, z + (1 if right else NZ - 1), c), device_id_type=MESH)

    def ag_wait_recv(k, s, right):
        sems = agr_sem if right else agl_sem
        blk = lax.rem(z - s - 1 + NZ, NZ) if right else lax.rem(z + s + 1, NZ)
        pltpu.make_async_remote_copy(
            src_ref=pre.at[k, blk], dst_ref=pre.at[k, blk], send_sem=sems.at[0, k, s], recv_sem=sems.at[1, k, s],
            device_id=dev(x, y, z + (1 if right else NZ - 1), c), device_id_type=MESH).wait_recv()

    def steps(k, right):
        return 4 if (k == 0) == right else 3

    for k in range(KCH):
        @pl.when(stays == 0)
        def _():
            tr_copy(k).wait_recv()

        ag_copy(k, 0, True).start()
        ag_copy(k, 0, False).start()

    def slot_copy(s):
        return pltpu.make_async_remote_copy(
            src_ref=slot_ref, dst_ref=slots.at[d], send_sem=sl_sem.at[s], recv_sem=slr_sem.at[d],
            device_id=source_of(s), device_id_type=MESH)

    def slot_send(s, carry):
        @pl.when(s != me_source)
        def _():
            slot_copy(s).start()

        return carry

    pl.semaphore_wait(near_sem.at[1], 7)
    lax.fori_loop(0, 32, slot_send, 0)

    @pl.when(stays == 1)
    def _():
        slots[d] = slot_ref[...]

    def ag_step(s):
        for k in range(KCH):
            for right in (True, False):
                if s < steps(k, right):
                    ag_wait_recv(k, s, right)
                    if s + 1 < steps(k, right):
                        ag_copy(k, s + 1, right).start()

    def g_wait(kind, h):
        src = {"r": (gr_sem, piece(x + 3, c, h)), "l": (gl_sem, piece(x + 1, c, h)), "f": (gf_sem, piece(x + 2, c, h))}
        sems, ref = src[kind]
        pltpu.make_async_remote_copy(
            src_ref=ref, dst_ref=ref, send_sem=sems.at[0, h], recv_sem=sems.at[1, h],
            device_id=dev(x + 1, y, z, c), device_id_type=MESH).wait_recv()

    def gp_wait(o, h):
        ref = piece(x + o, oc, h)
        pltpu.make_async_remote_copy(
            src_ref=ref, dst_ref=ref, send_sem=gp_sem.at[0, o, h], recv_sem=gp_sem.at[1, o, h],
            device_id=dev(x, y, z, oc), device_id_type=MESH).wait_recv()

    def g_near(h):
        g_wait("r", h)
        if h < 2:
            g_forward(h).start()
        g_partner(3, h).start()
        g_wait("l", h)
        if h >= 2:
            g_forward(h).start()
        g_partner(1, h).start()

    def g_far(h):
        g_wait("f", h)
        g_partner(2, h).start()

    def multiply(others, blocks, fresh):
        rows = [lax.rem(x + o, NX) for o in others]
        left = jnp.concatenate(
            [jnp.concatenate([gall[xx, zz, k] for zz in blocks for k in range(KCH)], axis=1) for xx in rows], axis=0)
        right = jnp.concatenate([pre[k, zz] for zz in blocks for k in range(KCH)], axis=1)
        part = lax.dot_general(left, right, (((1,), (1,)), ((), ())), preferred_element_type=F32)
        for i, xx in enumerate(rows):
            piece_of = part[i * 128 : (i + 1) * 128]
            acc[xx] = piece_of if fresh else acc[xx] + piece_of

    def out_copy(o, t):
        xx, xo = lax.rem(x + o, NX), lax.rem(x + t, NX)
        return pltpu.make_async_remote_copy(
            src_ref=out_s.at[xo, xx], dst_ref=out_r.at[y, xx], send_sem=os_sem.at[o, t], recv_sem=or_sem.at[y, xx],
            device_id=dev(xo, beta, z, c), device_id_type=MESH)

    def packed(o):
        xx = lax.rem(x + o, NX)
        rows = jnp.dot(pack[xx], acc[xx].astype(BF16), preferred_element_type=F32)
        out_s[:, xx] = rows.astype(BF16).reshape(NX, 64, 128)
        for t in (2, 1, 3):
            out_copy(o, t).start()

        @pl.when(stays == 0)
        def _():
            out_copy(o, 0).start()

        @pl.when(stays == 1)
        def _():
            out_r[y, xx] = out_s[x, xx]

    def away(*steps):
        return [lax.rem(z + r, NZ) for r in steps]

    g_near(0)
    g_near(1)
    ag_step(0)
    g_near(2)
    ag_step(1)
    g_near(3)
    ag_step(2)
    for o in (0, 1, 3):
        for h in range(4):
            gp_wait(o, h)
    multiply((0, 1, 3), away(0, 1, 7), True)
    multiply((0, 1, 3), away(2, 6), False)
    multiply((0, 1, 3), away(3, 5), False)
    g_far(0)
    g_far(2)
    upper = (lax.broadcasted_iota(I32, (128, 128), 0) < lax.broadcasted_iota(I32, (128, 128), 1)).astype(F32).astype(BF16)

    def slot_wait(o, carry):
        @pl.when(o != me_owner)
        def _():
            pltpu.make_async_remote_copy(
                src_ref=slot_ref, dst_ref=slots.at[o], send_sem=sl_sem.at[o], recv_sem=slr_sem.at[o],
                device_id=source_of(o), device_id_type=MESH).wait_recv()

        return carry

    lax.fori_loop(0, 32, slot_wait, 0)
    row = lax.broadcasted_iota(I32, (256, 128), 0)
    for xx in range(NX):
        hit = lax.shift_right_logical(slots[xx * NZ + z], 7) == lax.shift_right_logical(row, 3)
        rank = jnp.dot(hit.astype(F32).astype(BF16), upper, preferred_element_type=F32)
        pack[xx] = jnp.where(hit & (rank == (row & 7).astype(F32)), 1.0, 0.0).astype(BF16)
    for j in range(32):
        slot_rep[j * 8 : (j + 1) * 8, :] = jnp.broadcast_to(slots[(j % 4) * NZ + j // 4], (8, 128))
    rep = slot_rep[...]
    hit = lax.shift_right_logical(rep, 7) == d
    rank = jnp.dot(hit.astype(F32).astype(BF16), upper, preferred_element_type=F32)
    taken = jnp.where(hit & (rank == (row & 7).astype(F32)), (rep & 127).astype(F32) + 1.0, 0.0)
    target = jnp.sum(taken, axis=1, keepdims=True) - 1.0
    place[...] = jnp.where(
        target == lax.broadcasted_iota(I32, (256, 128), 1).astype(F32), 1.0, 0.0).astype(BF16)

    ag_step(3)
    multiply((0, 1, 3), away(4), False)
    for o in (0, 1, 3):
        packed(o)
    for i, h in enumerate((0, 2)):
        gp_wait(2, h)
        multiply((2,), (h, 4 + h), i == 0)
    g_far(1)
    g_far(3)
    for h in (1, 3):
        gp_wait(2, h)
        multiply((2,), (h, 4 + h), False)

    packed(2)

    for k in range(KCH):
        ex_copy(k).wait_send()
        for o in (1, 2, 3):
            rs_copy(k, o).wait_send()

        @pl.when(stays == 0)
        def _():
            tr_copy(k).wait_send()

        for right in (True, False):
            for s in range(steps(k, right)):
                ag_copy(k, s, right).wait_send()
    for h in range(4):
        g_right(h).wait_send()
        g_left(h).wait_send()
        g_forward(h).wait_send()
        for o in range(NX):
            g_partner(o, h).wait_send()

    def drain(i, carry):
        @pl.when(i != me_source)
        def _():
            slot_copy(i).wait_send()

        return carry

    lax.fori_loop(0, 32, drain, 0)

    def out_wait(ys):
        for xx in range(NX):
            pltpu.make_async_remote_copy(
                src_ref=out_s.at[0, xx], dst_ref=out_r.at[ys, xx], send_sem=os_sem.at[0, 0], recv_sem=or_sem.at[ys, xx],
                device_id=dev(2 * ys - y + NX, ys, z, c), device_id_type=MESH).wait_recv()

    for o in (1, 2, 3):
        out_wait(lax.rem(y + o, NY))

    @pl.when(stays == 0)
    def _():
        out_wait(y)

    total = out_r[0].astype(F32)
    for ys in range(1, NY):
        total += out_r[ys].astype(F32)
    total = total.reshape(NX, NZ, 8, 128)
    for zo in range(NZ):
        mid_s[zo] = jnp.concatenate([total[xx, zo] for xx in range(NX)], axis=0).astype(BF16)

    def mid_copy(o):
        zo = lax.rem(z + o, NZ)
        return pltpu.make_async_remote_copy(
            src_ref=mid_s.at[zo], dst_ref=mid_r.at[z], send_sem=ms_sem.at[o], recv_sem=mr_sem.at[z],
            device_id=dev(x, y, z + o, c), device_id_type=MESH)

    for o in (4, 3, 5, 2, 6, 1, 7):
        mid_copy(o).start()
    mid_r[z] = mid_s[z]
    for o in (1, 7, 2, 6, 3, 5, 4):
        zo = lax.rem(z + o, NZ)
        pltpu.make_async_remote_copy(
            src_ref=mid_s.at[zo], dst_ref=mid_r.at[zo], send_sem=ms_sem.at[o], recv_sem=mr_sem.at[zo],
            device_id=dev(x, y, z + o, c), device_id_type=MESH).wait_recv()
    out_ref[...] = lax.dot_general(
        place[...], mid_r[...].reshape(256, 128), (((0,), (0,)), ((), ())), preferred_element_type=F32)

    for o in range(NX):
        for t in (1, 2, 3):
            out_copy(o, t).wait_send()

        @pl.when(stays == 0)
        def _():
            out_copy(o, 0).wait_send()

    for o in range(1, NZ):
        mid_copy(o).wait_send()


def local(grads, scales, example_group, group_slot, inv_hess, queries):
    vmem = pl.BlockSpec(memory_space=pltpu.VMEM)
    hbm = pl.BlockSpec(memory_space=pltpu.HBM)
    dma = pltpu.SemaphoreType.DMA
    return pl.pallas_call(
        kernel,
        out_shape=jax.ShapeDtypeStruct((128, 128), F32),
        in_specs=[hbm] * 6,
        out_specs=vmem,
        scratch_shapes=[
            pltpu.VMEM((16, 1024), F32),
            pltpu.VMEM((1024, 16), F32),
            pltpu.VMEM((1, 1024), I32),
            pltpu.VMEM((1, 128), I32),
            pltpu.VMEM((2, 4, 128, 2048), BF16),
            pltpu.VMEM((KCH, 2048, CW), BF16),
            pltpu.VMEM((2, 1024, 1024), BF16),
            pltpu.VMEM((KCH, 4, 128, CW), BF16),
            pltpu.VMEM((KCH, 4, 128, CW), BF16),
            pltpu.VMEM((KCH, 4, 128, CW), F32),
            pltpu.VMEM((KCH, 4, 128, CW), BF16),
            pltpu.VMEM((KCH, 4, 128, CW), BF16),
            pltpu.VMEM((KCH, 128, CW), BF16),
            pltpu.VMEM((KCH, NZ, 128, CW), BF16),
            pltpu.VMEM((NX, NZ, KCH, 128, CW), BF16),
            pltpu.VMEM((NX, 128, 128), F32),
            pltpu.VMEM((32, 1, 128), I32),
            pltpu.VMEM((256, 128), I32),
            pltpu.VMEM((NX, 256, 128), BF16),
            pltpu.VMEM((256, 128), BF16),
            pltpu.VMEM((NX, NX, 64, 128), BF16),
            pltpu.VMEM((NY, NX, 64, 128), BF16),
            pltpu.VMEM((NZ, 32, 128), BF16),
            pltpu.VMEM((NZ, 32, 128), BF16),
            dma((15,)),
            pltpu.SemaphoreType.REGULAR((2,)),
            dma((2, KCH)),
            dma((KCH, 4)),
            dma((KCH, 4)),
            dma((2, KCH)),
            dma((2, KCH, 4)),
            dma((2, KCH, 4)),
            dma((2, 4)),
            dma((2, 4)),
            dma((2, 4)),
            dma((2, 4, 4)),
            dma((32,)),
            dma((32,)),
            dma((NX, NX)),
            dma((NY, NX)),
            dma((NZ,)),
            dma((NZ,)),
        ],
        compiler_params=pltpu.CompilerParams(collective_id=0, has_side_effects=True, vmem_limit_bytes=67_043_328),
        name="scores",
    )(grads, scales, example_group, group_slot.reshape(1, 128), inv_hess, queries)


def solution(mesh):
    in_specs = (P("dp", "mp"), P("mp", "dp"), P("dp", None), P("dp"), P("mp", "dp"), P(None, "mp"))
    out_specs = P("dp", "mp")
    return jax.shard_map(local, mesh=mesh, in_specs=in_specs, out_specs=out_specs, check_vma=False)
```
